32 devices in a mesh: seq: 8 (over z, y), dp: 4 (over x, core).
Axes of the slice: x: 2, y: 2, z: 4, core: 2. Of those that a mesh axis runs over, the one named last changes fastest.
Arguments:
- tokens: bfloat16 [4, 2048, 2048], P('dp', 'seq'), may hold values from -6 to 6
- query_weight: bfloat16 [2048, 2048], P(None, 'seq'), may hold values from -0.125 to 0.125
- key_rows: bfloat16 [4, 2048, 2048], P('dp', 'seq'), may hold values from -6 to 6
- value_rows: bfloat16 [4, 2048, 2048], P('dp', 'seq'), may hold values from -6 to 6
- out_grad: bfloat16 [4, 2048, 2048], P('dp', 'seq'), may hold values from -6 to 6
Outputs:
- attended: bfloat16 [4, 2048, 2048], P('dp', 'seq')
- key_grad: bfloat16 [4, 2048, 2048], P('dp', 'seq')
- value_grad: bfloat16 [4, 2048, 2048], P('dp', 'seq')
- weight_grad: float32 [2048, 2048], P('seq')
The draws below stay inside these ranges and needn't reach their ends.
All inputs are finite; a program needn't handle non-finite values.
Results may differ from the reference program's by a relative error of at most 0.0058.
Values may be sent and summed in bfloat16 or wider, within the bound.
No kernel may reach another device: no remote copies, remote signals or barrier semaphores. Data moves between devices by JAX's collectives and lax.ppermute only.
A program may use at most 320 MiB of HBM per device.

```python
import math
from functools import partial
import jax
import jax.numpy as jnp
from jax import lax

D = 2048
HEADS = 16
DH = 128
TOK_DEV = 256
LENGTH = 2048
BATCH = 4


def raised(values, rng, source, target, parts, factor):
    owner, partner = [(jnp.arange(values.shape[dim]) // (values.shape[dim] // parts)).reshape([-1 if axis == dim else 1 for axis in range(values.ndim)]) for dim in (source, target)]
    chosen = jax.random.permutation(rng, parts)[partner]
    strong = (owner == chosen) | (owner == (partner + parts // 2) % parts)
    return jnp.where(strong, factor * values, values)


def block_levels(own_key, dims, split, low, high):
    def one(position, parts):
        heights = jax.random.uniform(jax.random.fold_in(jax.random.fold_in(own_key, 6), position), (parts,), jnp.float32, low / len(split), high / len(split))
        return jnp.repeat(jnp.exp(heights), dims[position] // parts).reshape((-1,) + (1,) * (len(dims) - position - 1))

    level = one(*split[0])
    for cut in split[1:]:
        level = level * one(*cut)
    return level


def gaussian(rng, extent, deviation, most, shards=(), held_as=jnp.bfloat16):
    drawn = deviation * jax.random.normal(rng, extent, jnp.float32)
    if shards:
        drawn = drawn * block_levels(rng, extent, shards, -0.22, 0.18)
    return jnp.clip(drawn, -most, most).astype(held_as)


def gaussian_with(stream_key, extent, spread, reach, shards, heavy, kind=jnp.bfloat16):
    drawn = spread * jax.random.normal(stream_key, extent, jnp.float32)
    if shards:
        drawn = drawn * block_levels(stream_key, extent, shards, -0.22, 0.18)
    return jnp.clip(raised(drawn, jax.random.fold_in(stream_key, 3), *heavy), -reach, reach).astype(kind)


def setup_inputs(seed: int = 0) -> dict:
    key_of = jax.random.split(jax.random.key(seed), 6)
    return {
        "tokens": gaussian_with(key_of[0], (BATCH, LENGTH, D), 1.0, 6.0, ((0, 4), (1, 8)), (1, 2, 8, 2.0)),
        "query_weight": gaussian(key_of[1], (D, HEADS * DH), D ** -0.5, 0.125, ((1, 8),)),
        "key_rows": gaussian(key_of[2], (BATCH, LENGTH, HEADS * DH), 1.0, 6.0, ((0, 4), (1, 8))),
        "value_rows": gaussian(key_of[3], (BATCH, LENGTH, HEADS * DH), 1.0, 6.0, ((0, 4), (1, 8))),
        "out_grad": gaussian(key_of[4], (BATCH, LENGTH, HEADS * DH), 1.0, 6.0, ((0, 4), (1, 8))),
    }


def block_terms(block):
    query_rows, key_rows, value_rows, out_grad, prefix_state, suffix_state = block
    factor = 1.0 / math.sqrt(DH * LENGTH)
    row_count = query_rows.shape[0]
    query_heads = query_rows.reshape(row_count, HEADS, DH).astype(jnp.float32)
    key_heads = key_rows.reshape(row_count, HEADS, DH).astype(jnp.float32)
    value_heads = value_rows.reshape(row_count, HEADS, DH).astype(jnp.float32)
    grad_heads = out_grad.reshape(row_count, HEADS, DH).astype(jnp.float32)
    lower_mask = (jnp.arange(row_count)[:, None] >= jnp.arange(row_count)[None, :])[None]
    key_scores = jnp.where(lower_mask, factor * jnp.einsum('ihd,jhd->hij', query_heads, key_heads), 0.0)
    key_scores = lax.optimization_barrier(key_scores.astype(jnp.bfloat16)).astype(jnp.float32)
    grad_scores = jnp.where(lower_mask, factor * jnp.einsum('ihe,jhe->hij', grad_heads, value_heads), 0.0)
    grad_scores = lax.optimization_barrier(grad_scores.astype(jnp.bfloat16)).astype(jnp.float32)
    prefix_half = lax.optimization_barrier(prefix_state.astype(jnp.bfloat16)).astype(jnp.float32)
    suffix_half = lax.optimization_barrier(suffix_state.astype(jnp.bfloat16)).astype(jnp.float32)
    attended = jnp.einsum('hij,jhe->ihe', key_scores, value_heads) + factor * jnp.einsum('ihd,hde->ihe', query_heads, prefix_half)
    query_grad = jnp.einsum('hij,jhd->ihd', grad_scores, key_heads) + factor * jnp.einsum('ihe,hde->ihd', grad_heads, prefix_half)
    key_grad = jnp.einsum('hij,ihd->jhd', grad_scores, query_heads) + factor * jnp.einsum('jhe,hde->jhd', value_heads, suffix_half)
    value_grad = jnp.einsum('hij,ihe->jhe', key_scores, grad_heads) + factor * jnp.einsum('jhd,hde->jhe', key_heads, suffix_half)
    width = HEADS * DH
    return (attended.reshape(row_count, width).astype(jnp.bfloat16), query_grad.reshape(row_count, width).astype(jnp.bfloat16), key_grad.reshape(row_count, width).astype(jnp.bfloat16), value_grad.reshape(row_count, width).astype(jnp.bfloat16))

def one_sequence(query_weight, items):
    tokens, key_rows, value_rows, out_grad = items
    query_rows = jnp.dot(tokens, query_weight, preferred_element_type=jnp.float32).astype(jnp.bfloat16)
    block_count = LENGTH // TOK_DEV

    def split_rows(array):
        return array.reshape(block_count, TOK_DEV, HEADS * DH)

    def heads_wide(array):
        return array.reshape(block_count, TOK_DEV, HEADS, DH).astype(jnp.float32)
    block_kv = jnp.einsum('crhd,crhe->chde', heads_wide(key_rows), heads_wide(value_rows))
    block_qg = jnp.einsum('crhd,crhe->chde', heads_wide(query_rows), heads_wide(out_grad))
    zero_state = jnp.zeros((1, HEADS, DH, DH), jnp.float32)
    prefix_state = jnp.concatenate([zero_state, jnp.cumsum(block_kv, axis=0)[:-1]], axis=0)
    suffix_state = jnp.concatenate([jnp.cumsum(block_qg[::-1], axis=0)[::-1][1:], zero_state], axis=0)
    attended, query_grad, key_grad, value_grad = lax.map(block_terms, (split_rows(query_rows), split_rows(key_rows), split_rows(value_rows), split_rows(out_grad), prefix_state, suffix_state))
    width = HEADS * DH
    query_grad = query_grad.reshape(LENGTH, width)
    weight_part = jnp.dot(tokens.T, query_grad, preferred_element_type=jnp.float32)
    return (attended.reshape(LENGTH, width), key_grad.reshape(LENGTH, width), value_grad.reshape(LENGTH, width), weight_part)

def reference(tokens, query_weight, key_rows, value_rows, out_grad):
    attended, key_grad, value_grad, weight_parts = lax.map(partial(one_sequence, query_weight), (tokens, key_rows, value_rows, out_grad))
    return (attended, key_grad, value_grad, lax.optimization_barrier(jnp.sum(weight_parts, axis=0)))
```

```python
import functools
import math

import jax
import jax.numpy as jnp
from jax import lax
from jax.experimental import pallas as pl
from jax.experimental.pallas import tpu as pltpu
from jax.sharding import PartitionSpec as P

DH = 128
F32 = jnp.float32
BF16 = jnp.bfloat16
MIB = 1 << 20


def dot(a, b, dims):
    return lax.dot_general(a, b, ((dims[:1], dims[1:]), ((), ())), preferred_element_type=F32)


def lanes(index, width=DH):
    return pl.ds(pl.multiple_of(index * width, DH), width)


def call(kernel, outs, *args, flops=0):
    moved = sum(math.prod(a.shape) * a.dtype.itemsize for a in (*args, *outs))
    return pl.pallas_call(
        kernel,
        out_shape=tuple(outs),
        in_specs=[pl.BlockSpec(memory_space=pltpu.VMEM)] * len(args),
        out_specs=tuple([pl.BlockSpec(memory_space=pltpu.VMEM)] * len(outs)),
        cost_estimate=pl.CostEstimate(flops=flops, bytes_accessed=moved, transcendentals=0),
        compiler_params=pltpu.CompilerParams(vmem_limit_bytes=min(60 * MIB, 2 * moved + 8 * MIB)),
    )(*args)


def out(shape, dtype):
    return jax.ShapeDtypeStruct(shape, dtype)


def causal(rows):
    return lax.broadcasted_iota(jnp.int32, (rows, rows), 0) >= lax.broadcasted_iota(
        jnp.int32, (rows, rows), 1
    )


def scores(a, b, mask, factor):
    return jnp.where(mask, factor * dot(a, b, (1, 1)), 0.0).astype(BF16)


def head_of(slot, shards, interleaved):
    if not interleaved:
        return slot
    s, d = lax.axis_index("seq"), lax.axis_index("dp")
    half, rest = divmod(slot, shards)
    step, side = divmod(rest, 2)
    source = lax.rem(s // 2 + (shards // 2 - step), shards // 2) * 2 + lax.rem(s + side, 2)
    return source * 2 + lax.rem(d // 2 + half, 2)


def kv_kernel(heads, k_ref, v_ref, o_ref):
    for h in range(heads):
        cols = pl.ds(h * DH, DH)
        o_ref[pl.ds(h * DH, DH), :] = dot(k_ref[:, cols], v_ref[:, cols], (0, 0)).astype(BF16)


def qg_kernel(heads, shards, inter, qa_ref, qb_ref, g_ref, o_ref):
    for slot in range(heads):
        ref = (qa_ref, qb_ref)[slot // (heads // 2)]
        h = head_of(slot, shards, inter)
        q = ref[:, pl.ds(slot % (heads // 2) * DH, DH)]
        o_ref[lanes(h), :] = dot(q, g_ref[:, lanes(h)], (0, 0)).astype(BF16)


def scan_kernel(count, backward, i_ref, o_ref):
    rows = i_ref.shape[0] // count
    total = jnp.zeros((rows, i_ref.shape[1]), F32)
    order = range(count)
    for c in reversed(order) if backward else order:
        block = pl.ds(c * rows, rows)
        o_ref[block, :] = total.astype(BF16)
        total = total + i_ref[block, :].astype(F32)


def query_grad_kernel(factor, heads, k_ref, v_ref, g_ref, p_ref, *o_refs):
    mask = causal(k_ref.shape[0])
    d = lax.axis_index("dp")
    per = heads // len(o_refs)
    for step, o_ref in enumerate(o_refs):
        base = jnp.bitwise_xor(d, step) * per
        for j in range(per):
            cols = lanes(base + j)
            g = g_ref[:, cols]
            grad_scores = scores(g, v_ref[:, cols], mask, factor)
            o_ref[:, pl.ds(j * DH, DH)] = (
                dot(grad_scores, k_ref[:, cols], (1, 0))
                + factor * dot(g, p_ref[cols, :], (1, 1))
            ).astype(BF16)


def attended_kernel(factor, heads, shards, inter, qa_ref, qb_ref, k_ref, v_ref, p_ref, o_ref):
    mask = causal(k_ref.shape[0])
    for slot in range(heads):
        ref = (qa_ref, qb_ref)[slot // (heads // 2)]
        cols = lanes(head_of(slot, shards, inter))
        q = ref[:, pl.ds(slot % (heads // 2) * DH, DH)]
        key_scores = scores(q, k_ref[:, cols], mask, factor)
        o_ref[:, cols] = (
            dot(key_scores, v_ref[:, cols], (1, 0)) + factor * dot(q, p_ref[cols, :], (1, 0))
        ).astype(BF16)


def pair_grad_kernel(
    factor, heads, shards, inter, qa_ref, qb_ref, k_ref, v_ref, g_ref, s_ref, dk_ref, dv_ref
):
    mask = causal(k_ref.shape[0])
    for slot in range(heads):
        ref = (qa_ref, qb_ref)[slot // (heads // 2)]
        cols = lanes(head_of(slot, shards, inter))
        q = ref[:, pl.ds(slot % (heads // 2) * DH, DH)]
        k, v, g, suffix = k_ref[:, cols], v_ref[:, cols], g_ref[:, cols], s_ref[cols, :]
        key_scores = scores(q, k, mask, factor)
        grad_scores = scores(g, v, mask, factor)
        dk_ref[:, cols] = (
            dot(grad_scores, q, (0, 0)) + factor * dot(v, suffix, (1, 1))
        ).astype(BF16)
        dv_ref[:, cols] = (
            dot(key_scores, g, (0, 0)) + factor * dot(k, suffix, (1, 0))
        ).astype(BF16)


def project_kernel(mine_ref, theirs_ref, near_ref, far_ref, qa_ref, qb_ref):
    depth = near_ref.shape[1]
    c = lax.rem(lax.axis_index("dp"), 2)
    width = near_ref.shape[2]
    for t_ref, o_ref in ((mine_ref, qa_ref), (theirs_ref, qb_ref)):
        near = t_ref[:, lanes(c, depth)]
        far = t_ref[:, lanes(1 - c, depth)]
        for step in range(near_ref.shape[0]):
            o_ref[:, pl.ds(step * width, width)] = (
                dot(near, near_ref[step], (1, 0)) + dot(far, far_ref[step], (1, 0))
            ).astype(BF16)


def weight_kernel(count, other, *refs):
    o_ref = refs[-1]
    pairs = len(refs) // 2
    rows = refs[0].shape[1] // count
    s = lax.axis_index("seq")
    for step in range(count // 2):
        target = lax.rem(s // 2 + step, count // 2) * 2 + lax.rem(s + other, 2)
        total = None
        for t_ref, g_ref in zip(refs[:pairs], refs[pairs:-1]):
            term = dot(t_ref[:, lanes(target, rows)], g_ref[...], (0, 0))
            total = term if total is None else total + term
        o_ref[pl.ds(step * rows, rows), :] = total.astype(o_ref.dtype)


def fold_kernel(keep_ref, got_ref, *o_refs):
    rows = o_refs[0].shape[0]
    for step, o_ref in enumerate(o_refs):
        block = pl.ds(step * rows, rows)
        o_ref[...] = (keep_ref[block, :] + got_ref[block, :].astype(F32)).astype(o_ref.dtype)


def sum_kernel(first_ref, *refs):
    total = first_ref[...]
    for ref in refs[:-1]:
        total = total + ref[...].astype(F32)
    refs[-1][...] = total.astype(refs[-1].dtype)


def join_kernel(*refs):
    d = lax.axis_index("dp")
    width = refs[0].shape[1]
    for step, ref in enumerate(refs[:-1]):
        refs[-1][:, lanes(jnp.bitwise_xor(d, step), width)] = ref[...].astype(F32)


def body(tokens, query_weight, key_rows, value_rows, out_grad):
    rows, width = key_rows.shape[1:]
    model = tokens.shape[2]
    heads = width // DH
    seqs, dps = lax.axis_size("seq"), lax.axis_size("dp")
    factor = 1.0 / math.sqrt(DH * rows * seqs)
    split = query_weight.shape[1] == 2 * DH and seqs == 8 and dps == 4
    toks, keys, values, grads = tokens[0], key_rows[0], value_rows[0], out_grad[0]
    state = out((heads * DH, DH), BF16)

    def xor_dp(value, step):
        return lax.ppermute(value, "dp", [(i, i ^ step) for i in range(dps)])

    def flip_seq(value):
        return lax.ppermute(value, "seq", [(i, i ^ 1) for i in range(seqs)])

    def turn_seq(value, step):
        return lax.ppermute(value, "seq", [(i, (i + 2 * step) % seqs) for i in range(seqs)])

    def swap(value):
        return lax.all_to_all(value, "seq", 0, 0, tiled=True)

    def carried(blocks, backward):
        scan = functools.partial(scan_kernel, seqs, backward)
        return swap(call(scan, [state], swap(blocks))[0])

    group = [toks] + [xor_dp(toks, step) for step in (1, 2) if step < dps]
    if split:
        group.append(xor_dp(group[2], 1))
    else:
        group += [xor_dp(toks, step) for step in range(3, dps)]

    if split:
        d = lax.axis_index("dp")
        half = model // 2
        piece = lax.dynamic_slice(query_weight, (d % 2 * half, d // 2 * DH), (half, DH))
        column = [piece] + [turn_seq(piece, step) for step in range(1, seqs // 2)]
        sides = [flip_seq(value) for value in column]
        near = jnp.stack([jnp.concatenate(two, axis=1) for two in zip(column, sides)])
        far = xor_dp(near, 1)
        qs = call(
            project_kernel,
            [out((rows, width // 2), BF16)] * 2,
            toks,
            group[2],
            near,
            far,
            flops=2 * rows * model * width,
        )
        pair = (qs[0], xor_dp(qs[1], 2))
    else:
        query_rows = jnp.dot(
            toks,
            lax.all_gather(query_weight, "seq", axis=1, tiled=True),
            preferred_element_type=F32,
        ).astype(BF16)
        pair = (query_rows[:, : width // 2], query_rows[:, width // 2 :])

    block_kv = call(functools.partial(kv_kernel, heads), [state], keys, values)[0]
    prefix = carried(block_kv, False)
    grad_parts = call(
        functools.partial(query_grad_kernel, factor, heads),
        [out((rows, width // dps), BF16)] * dps,
        keys,
        values,
        grads,
        prefix,
    )
    grad_group = [grad_parts[0]] + [xor_dp(grad_parts[step], step) for step in range(1, dps)]

    if split:
        block = model // seqs
        tall = (model // 2, width // dps)
        send = call(
            functools.partial(weight_kernel, seqs, 1),
            [out(tall, BF16)],
            *group,
            *grad_group,
        )[0]
        got = flip_seq(send)
        keep = call(
            functools.partial(weight_kernel, seqs, 0),
            [out(tall, F32)],
            *group,
            *grad_group,
        )[0]
        folded = call(
            fold_kernel,
            [out((block, tall[1]), F32 if step == 0 else BF16) for step in range(seqs // 2)],
            keep,
            got,
        )
        share = call(
            sum_kernel,
            [out((block, tall[1]), BF16)],
            folded[0],
            *[turn_seq(folded[step], step) for step in range(1, seqs // 2)],
        )[0]
    else:
        share = lax.psum_scatter(
            lax.dot_general(
                jnp.concatenate(group),
                jnp.concatenate(grad_group),
                (((0,), (0,)), ((), ())),
                preferred_element_type=F32,
            ),
            "seq",
            scatter_dimension=0,
            tiled=True,
        )
    weight_grad = call(
        join_kernel,
        [out((share.shape[0], width), F32)],
        share,
        *[xor_dp(share, step) for step in range(1, dps)],
    )[0]

    block_qg = call(
        functools.partial(qg_kernel, heads, seqs, split), [state], *pair, grads
    )[0]
    suffix = carried(block_qg, True)
    attended = call(
        functools.partial(attended_kernel, factor, heads, seqs, split),
        [out((rows, width), BF16)],
        *pair,
        keys,
        values,
        prefix,
    )[0]
    key_grad, value_grad = call(
        functools.partial(pair_grad_kernel, factor, heads, seqs, split),
        [out((rows, width), BF16)] * 2,
        *pair,
        keys,
        values,
        grads,
        suffix,
    )
    return (attended[None], key_grad[None], value_grad[None], weight_grad)


def solution(mesh):
    return jax.shard_map(
        body,
        mesh=mesh,
        in_specs=(
            P("dp", "seq", None),
            P(None, "seq"),
            P("dp", "seq", None),
            P("dp", "seq", None),
            P("dp", "seq", None),
        ),
        out_specs=(
            P("dp", "seq", None),
            P("dp", "seq", None),
            P("dp", "seq", None),
            P("seq", None),
        ),
        check_vma=False,
    )
```

```python
import functools
import math

import jax
import jax.numpy as jnp
from jax import lax
from jax.experimental import pallas as pl
from jax.experimental.pallas import tpu as pltpu
from jax.sharding import PartitionSpec as P


DH = 128
F32 = jnp.float32
BF16 = jnp.bfloat16
MIB = 1 << 20


def dot(a, b, dims):
    return lax.dot_general(a, b, ((dims[:1], dims[1:]), ((), ())), preferred_element_type=F32)


def lanes(index, width=DH):
    return pl.ds(pl.multiple_of(index * width, DH), width)


def call(kernel, outs, *args, flops=0, scratch=()):
    moved = sum(math.prod(a.shape) * a.dtype.itemsize for a in (*args, *outs))
    return pl.pallas_call(
        kernel,
        out_shape=tuple(outs),
        in_specs=[pl.BlockSpec(memory_space=pltpu.VMEM)] * len(args),
        out_specs=tuple([pl.BlockSpec(memory_space=pltpu.VMEM)] * len(outs)),
        scratch_shapes=[pltpu.VMEM(a.shape, a.dtype) for a in scratch],
        cost_estimate=pl.CostEstimate(flops=flops, bytes_accessed=moved, transcendentals=0),
        compiler_params=pltpu.CompilerParams(vmem_limit_bytes=min(60 * MIB, 2 * moved + 8 * MIB)),
    )(*args)


def out(shape, dtype):
    return jax.ShapeDtypeStruct(shape, dtype)


def causal(rows):
    return lax.broadcasted_iota(jnp.int32, (rows, rows), 0) >= lax.broadcasted_iota(
        jnp.int32, (rows, rows), 1
    )


def scores(a, b, mask, factor):
    return jnp.where(mask, factor * dot(a, b, (1, 1)), 0.0).astype(BF16)


def head_of(slot, shards, interleaved):
    if not interleaved:
        return slot
    s, d = lax.axis_index("seq"), lax.axis_index("dp")
    half, rest = divmod(slot, shards)
    step, side = divmod(rest, 2)
    source = lax.rem(s // 2 + (shards // 2 - step), shards // 2) * 2 + lax.rem(s + side, 2)
    return source * 2 + lax.rem(d // 2 + half, 2)


def kv_kernel(heads, k_ref, v_ref, *o_refs):
    y = lax.rem(lax.axis_index("seq"), 2)
    per = heads // len(o_refs)
    for part, o_ref in enumerate(o_refs):
        for j in range(per):
            h = j if len(o_refs) == 1 else lax.rem(y + part, 2) * per + j
            cols = lanes(h)
            o_ref[pl.ds(j * DH, DH), :] = dot(k_ref[:, cols], v_ref[:, cols], (0, 0)).astype(
                o_ref.dtype
            )


def qg_kernel(heads, shards, inter, qa_ref, qb_ref, g_ref, *o_refs):
    y = lax.rem(lax.axis_index("seq"), 2)
    total_ref = o_refs[-1]
    for slot in range(heads):
        ref = (qa_ref, qb_ref)[slot // (heads // 2)]
        h = head_of(slot, shards, inter)
        q = ref[:, pl.ds(slot % (heads // 2) * DH, DH)]
        total_ref[lanes(h), :] = dot(q, g_ref[:, lanes(h)], (0, 0)).astype(total_ref.dtype)
    half = total_ref.shape[0] // 2
    for part, o_ref in enumerate(o_refs[:-1]):
        o_ref[...] = total_ref[lanes(lax.rem(y + part, 2), half), :].astype(o_ref.dtype)


def pair_kernel(keep_ref, got_ref, o_ref):
    o_ref[...] = (keep_ref[...] + got_ref[...].astype(F32)).astype(BF16)


def quad_kernel(keep_ref, got_ref, pair_ref, o_ref):
    o_ref[...] = (
        keep_ref[...] + got_ref[...].astype(F32) + pair_ref[...].astype(F32)
    ).astype(BF16)


def carry_kernel(backward, keep_ref, got_ref, pair_ref, quad_ref, mine_ref, theirs_ref):
    s = lax.axis_index("seq")
    y, z = lax.rem(s, 2), lax.rem(s // 2, 2)
    later = 0 if backward else 1
    base = quad_ref[...].astype(F32) + jnp.where(z == later, pair_ref[...].astype(F32), 0.0)
    mine_ref[...] = (base + jnp.where(y == later, got_ref[...].astype(F32), 0.0)).astype(BF16)
    theirs_ref[...] = (base + jnp.where(y == later, 0.0, keep_ref[...])).astype(BF16)


def whole_state(refs):
    if len(refs) == 1:
        return refs[0]
    mine_ref, other_ref, all_ref = refs
    y = lax.rem(lax.axis_index("seq"), 2)
    half = mine_ref.shape[0]
    all_ref[lanes(y, half), :] = mine_ref[...]
    all_ref[lanes(1 - y, half), :] = other_ref[...]
    return all_ref


def scan_kernel(count, backward, i_ref, o_ref):
    rows = i_ref.shape[0] // count
    total = jnp.zeros((rows, i_ref.shape[1]), F32)
    order = range(count)
    for c in reversed(order) if backward else order:
        block = pl.ds(c * rows, rows)
        o_ref[block, :] = total.astype(BF16)
        total = total + i_ref[block, :].astype(F32)


def query_grad_kernel(factor, heads, states, k_ref, v_ref, g_ref, *refs):
    o_refs = refs[states : len(refs) - states + 1]
    p_ref = whole_state(refs[:states] + refs[len(refs) - states + 1 :])
    mask = causal(k_ref.shape[0])
    d = lax.axis_index("dp")
    per = heads // len(o_refs)
    for step, o_ref in enumerate(o_refs):
        base = jnp.bitwise_xor(d, step) * per
        for j in range(per):
            cols = lanes(base + j)
            g = g_ref[:, cols]
            grad_scores = scores(g, v_ref[:, cols], mask, factor)
            o_ref[:, pl.ds(j * DH, DH)] = (
                dot(grad_scores, k_ref[:, cols], (1, 0))
                + factor * dot(g, p_ref[cols, :], (1, 1))
            ).astype(BF16)


def attended_kernel(factor, heads, states, shards, inter, qa_ref, qb_ref, k_ref, v_ref, *refs):
    o_ref = refs[states]
    p_ref = whole_state(refs[:states] + refs[states + 1 :])
    mask = causal(k_ref.shape[0])
    for slot in range(heads):
        ref = (qa_ref, qb_ref)[slot // (heads // 2)]
        cols = lanes(head_of(slot, shards, inter))
        q = ref[:, pl.ds(slot % (heads // 2) * DH, DH)]
        key_scores = scores(q, k_ref[:, cols], mask, factor)
        o_ref[:, cols] = (
            dot(key_scores, v_ref[:, cols], (1, 0)) + factor * dot(q, p_ref[cols, :], (1, 0))
        ).astype(BF16)


def pair_grad_kernel(
    factor, heads, states, shards, inter, qa_ref, qb_ref, k_ref, v_ref, g_ref, *refs
):
    dk_ref, dv_ref = refs[states : states + 2]
    s_ref = whole_state(refs[:states] + refs[states + 2 :])
    mask = causal(k_ref.shape[0])
    for slot in range(heads):
        ref = (qa_ref, qb_ref)[slot // (heads // 2)]
        cols = lanes(head_of(slot, shards, inter))
        q = ref[:, pl.ds(slot % (heads // 2) * DH, DH)]
        k, v, g, suffix = k_ref[:, cols], v_ref[:, cols], g_ref[:, cols], s_ref[cols, :]
        key_scores = scores(q, k, mask, factor)
        grad_scores = scores(g, v, mask, factor)
        dk_ref[:, cols] = (
            dot(grad_scores, q, (0, 0)) + factor * dot(v, suffix, (1, 1))
        ).astype(BF16)
        dv_ref[:, cols] = (
            dot(key_scores, g, (0, 0)) + factor * dot(k, suffix, (1, 0))
        ).astype(BF16)


def project_kernel(mine_ref, theirs_ref, near_ref, far_ref, qa_ref, qb_ref):
    depth = near_ref.shape[1]
    c = lax.rem(lax.axis_index("dp"), 2)
    width = near_ref.shape[2]
    for t_ref, o_ref in ((mine_ref, qa_ref), (theirs_ref, qb_ref)):
        near = t_ref[:, lanes(c, depth)]
        far = t_ref[:, lanes(1 - c, depth)]
        for step in range(near_ref.shape[0]):
            o_ref[:, pl.ds(step * width, width)] = (
                dot(near, near_ref[step], (1, 0)) + dot(far, far_ref[step], (1, 0))
            ).astype(BF16)


def weight_kernel(count, other, steps, *refs):
    o_ref = refs[-1]
    pairs = len(refs) // 2
    rows = refs[0].shape[1] // count
    s = lax.axis_index("seq")
    for place, step in enumerate(steps):
        target = lax.rem(s // 2 + step, count // 2) * 2 + lax.rem(s + other, 2)
        total = None
        for t_ref, g_ref in zip(refs[:pairs], refs[pairs:-1]):
            term = dot(t_ref[:, lanes(target, rows)], g_ref[...], (0, 0))
            total = term if total is None else total + term
        o_ref[pl.ds(place * rows, rows), :] = total.astype(o_ref.dtype)


def fold_kernel(start, keep_ref, got_ref, *o_refs):
    rows = o_refs[0].shape[0]
    for place, o_ref in enumerate(o_refs):
        kept = keep_ref[pl.ds((start + place) * rows, rows), :]
        o_ref[...] = (kept + got_ref[pl.ds(place * rows, rows), :].astype(F32)).astype(o_ref.dtype)


def sum_kernel(first_ref, *refs):
    total = first_ref[...]
    for ref in refs[:-1]:
        total = total + ref[...].astype(F32)
    refs[-1][...] = total.astype(refs[-1].dtype)


def join_kernel(*refs):
    d = lax.axis_index("dp")
    width = refs[0].shape[1]
    for step, ref in enumerate(refs[:-1]):
        refs[-1][:, lanes(jnp.bitwise_xor(d, step), width)] = ref[...].astype(F32)


def body(tokens, query_weight, key_rows, value_rows, out_grad):
    rows, width = key_rows.shape[1:]
    model = tokens.shape[2]
    heads = width // DH
    seqs, dps = lax.axis_size("seq"), lax.axis_size("dp")
    factor = 1.0 / math.sqrt(DH * rows * seqs)
    split = splits(query_weight.shape[1], seqs, dps)
    toks, keys, values, grads = tokens[0], key_rows[0], value_rows[0], out_grad[0]
    state = out((heads * DH, DH), BF16)

    def xor_dp(value, step):
        return lax.ppermute(value, "dp", [(i, i ^ step) for i in range(dps)])

    def flip_seq(value):
        return lax.ppermute(value, "seq", [(i, i ^ 1) for i in range(seqs)])

    def turn_seq(value, step):
        return lax.ppermute(value, "seq", [(i, (i + 2 * step) % seqs) for i in range(seqs)])

    def swap(value):
        return lax.all_to_all(value, "seq", 0, 0, tiled=True)

    def carried(blocks, backward):
        if not split:
            scan = functools.partial(scan_kernel, seqs, backward)
            got = swap(blocks[0])
            return [swap(call(scan, [state], got)[0])]
        keep, send = blocks
        part = out(send.shape, BF16)
        got = flip_seq(send)
        pair = call(pair_kernel, [part], keep, got)[0]
        pair = lax.ppermute(pair, "seq", [(i, i ^ 2) for i in range(seqs)])
        quad = call(quad_kernel, [part], keep, got, pair)[0]
        low, high = range(4), range(4, 8)
        quad = lax.ppermute(
            quad, "seq", list(zip(high, low) if backward else zip(low, high))
        )
        mine, theirs = call(
            functools.partial(carry_kernel, backward), [part, part], keep, got, pair, quad
        )
        return [mine, flip_seq(theirs)]

    half_state = (heads * DH // 2, DH)
    halves = [out(half_state, F32), out(half_state, BF16)] if split else [state]
    scratch = [state] if split else []
    states = len(halves)

    group = [toks] + [xor_dp(toks, step) for step in (1, 2) if step < dps]
    if split:
        group.append(xor_dp(group[2], 1))
    else:
        group += [xor_dp(toks, step) for step in range(3, dps)]

    block_kv = call(functools.partial(kv_kernel, heads), halves, keys, values)
    prefix = carried(block_kv, False)

    if split:
        d = lax.axis_index("dp")
        half = model // 2
        piece = lax.dynamic_slice(query_weight, (d % 2 * half, d // 2 * DH), (half, DH))
        column = [piece] + [turn_seq(piece, k) for k in range(1, seqs // 2)]
        sides = [flip_seq(value) for value in column]
        near = jnp.stack([jnp.concatenate(two, axis=1) for two in zip(column, sides)])
        far = xor_dp(near, 1)
        qs = call(
            project_kernel,
            [out((rows, width // 2), BF16)] * 2,
            toks,
            group[2],
            near,
            far,
            flops=2 * rows * model * width,
        )
        pair = (qs[0], xor_dp(qs[1], 2))
    else:
        query_rows = jnp.dot(
            toks,
            lax.all_gather(query_weight, "seq", axis=1, tiled=True),
            preferred_element_type=F32,
        ).astype(BF16)
        pair = (query_rows[:, : width // 2], query_rows[:, width // 2 :])

    grad_parts = call(
        functools.partial(query_grad_kernel, factor, heads, states),
        [out((rows, width // dps), BF16)] * dps,
        keys,
        values,
        grads,
        *prefix,
        scratch=scratch,
    )
    grad_group = [grad_parts[0]] + [xor_dp(grad_parts[step], step) for step in range(1, dps)]

    if split:
        block = (model // seqs, width // dps)
        cuts = ((2, 1), (3, 0))
        weights = (*group, *grad_group)
        gots = []
        for steps in cuts:
            send = call(
                functools.partial(weight_kernel, seqs, 1, steps),
                [out((len(steps) * block[0], block[1]), BF16)],
                *weights,
            )[0]
            gots.append(flip_seq(send))
        keep = call(
            functools.partial(weight_kernel, seqs, 0, sum(cuts, ())),
            [out((model // 2, block[1]), F32)],
            *weights,
        )[0]
        terms = []
        for part, steps in enumerate(cuts):
            folded = call(
                functools.partial(fold_kernel, part * len(steps)),
                [out(block, BF16 if step else F32) for step in steps],
                keep,
                gots[part],
            )
            for step, value in zip(steps, folded):
                terms.append(turn_seq(value, step) if step else value)
        share = call(sum_kernel, [out(block, BF16)], *terms[::-1])[0]
    else:
        share = lax.psum_scatter(
            lax.dot_general(
                jnp.concatenate(group),
                jnp.concatenate(grad_group),
                (((0,), (0,)), ((), ())),
                preferred_element_type=F32,
            ),
            "seq",
            scatter_dimension=0,
            tiled=True,
        )
    weight_grad = call(
        join_kernel,
        [out((share.shape[0], width), F32)],
        share,
        *[xor_dp(share, step) for step in range(1, dps)],
    )[0]

    block_qg = call(
        functools.partial(qg_kernel, heads, seqs, split),
        halves,
        *pair,
        grads,
        scratch=[out((heads * DH, DH), F32)] if split else [],
    )
    suffix = carried(block_qg, True)
    attended = call(
        functools.partial(attended_kernel, factor, heads, states, seqs, split),
        [out((rows, width), BF16)],
        *pair,
        keys,
        values,
        *prefix,
        scratch=scratch,
    )[0]
    key_grad, value_grad = call(
        functools.partial(pair_grad_kernel, factor, heads, states, seqs, split),
        [out((rows, width), BF16)] * 2,
        *pair,
        keys,
        values,
        grads,
        *suffix,
        scratch=scratch,
    )
    return (attended[None], key_grad[None], value_grad[None], weight_grad)


def splits(columns, seqs, dps):
    return columns == 2 * DH and seqs == 8 and dps == 4


def solution(mesh):
    step = jax.shard_map(
        body,
        mesh=mesh,
        in_specs=(
            P("dp", "seq", None),
            P(None, "seq"),
            P("dp", "seq", None),
            P("dp", "seq", None),
            P("dp", "seq", None),
        ),
        out_specs=(
            P("dp", "seq", None),
            P("dp", "seq", None),
            P("dp", "seq", None),
            P("seq", None),
        ),
        check_vma=False,
    )
    if dict(mesh.shape) == {"seq": 8, "dp": 4}:
        return step
    return step
```

```python
import functools
import math

import jax
import jax.numpy as jnp
from jax import lax
from jax.experimental import pallas as pl
from jax.experimental.pallas import tpu as pltpu
from jax.sharding import PartitionSpec as P


DH = 128
F32 = jnp.float32
BF16 = jnp.bfloat16
MIB = 1 << 20


def dot(a, b, dims):
    return lax.dot_general(a, b, ((dims[:1], dims[1:]), ((), ())), preferred_element_type=F32)


def lanes(index, width=DH):
    return pl.ds(pl.multiple_of(index * width, DH), width)


def call(kernel, outs, *args, flops=0, scratch=()):
    moved = sum(math.prod(a.shape) * a.dtype.itemsize for a in (*args, *outs))
    return pl.pallas_call(
        kernel,
        out_shape=tuple(outs),
        in_specs=[pl.BlockSpec(memory_space=pltpu.VMEM)] * len(args),
        out_specs=tuple([pl.BlockSpec(memory_space=pltpu.VMEM)] * len(outs)),
        scratch_shapes=[pltpu.VMEM(a.shape, a.dtype) for a in scratch],
        cost_estimate=pl.CostEstimate(flops=flops, bytes_accessed=moved, transcendentals=0),
        compiler_params=pltpu.CompilerParams(vmem_limit_bytes=min(60 * MIB, 2 * moved + 8 * MIB)),
    )(*args)


def out(shape, dtype):
    return jax.ShapeDtypeStruct(shape, dtype)


def causal(rows):
    return lax.broadcasted_iota(jnp.int32, (rows, rows), 0) >= lax.broadcasted_iota(
        jnp.int32, (rows, rows), 1
    )


def scores(a, b, mask, factor):
    return jnp.where(mask, factor * dot(a, b, (1, 1)), 0.0).astype(BF16)


def head_of(slot, shards, interleaved):
    if not interleaved:
        return slot
    s, d = lax.axis_index("seq"), lax.axis_index("dp")
    half, rest = divmod(slot, shards)
    step, side = divmod(rest, 2)
    source = jnp.bitwise_xor(s, step * 2 + side)
    return source * 2 + lax.rem(d // 2 + half, 2)


def kv_kernel(heads, k_ref, v_ref, *o_refs):
    y = lax.rem(lax.axis_index("seq"), 2)
    per = heads // len(o_refs)
    for part, o_ref in enumerate(o_refs):
        for j in range(per):
            h = j if len(o_refs) == 1 else lax.rem(y + part, 2) * per + j
            cols = lanes(h)
            o_ref[pl.ds(j * DH, DH), :] = dot(k_ref[:, cols], v_ref[:, cols], (0, 0)).astype(
                o_ref.dtype
            )


def qg_kernel(heads, shards, inter, count, *refs):
    q_refs, g_ref, o_refs = refs[:count], refs[count], refs[count + 1 :]
    y = lax.rem(lax.axis_index("seq"), 2)
    total_ref = o_refs[-1]
    for slot in range(heads):
        ref = q_refs[slot * count // heads]
        h = head_of(slot, shards, inter)
        q = ref[:, pl.ds(slot % (heads // count) * DH, DH)]
        total_ref[lanes(h), :] = dot(q, g_ref[:, lanes(h)], (0, 0)).astype(total_ref.dtype)
    half = total_ref.shape[0] // 2
    for part, o_ref in enumerate(o_refs[:-1]):
        o_ref[...] = total_ref[lanes(lax.rem(y + part, 2), half), :].astype(o_ref.dtype)


def pair_kernel(keep_ref, got_ref, o_ref):
    o_ref[...] = (keep_ref[...] + got_ref[...].astype(F32)).astype(BF16)


def quad_kernel(keep_ref, got_ref, pair_ref, o_ref):
    o_ref[...] = (
        keep_ref[...] + got_ref[...].astype(F32) + pair_ref[...].astype(F32)
    ).astype(BF16)


def carry_kernel(backward, keep_ref, got_ref, pair_ref, quad_ref, mine_ref, theirs_ref):
    s = lax.axis_index("seq")
    y, z = lax.rem(s, 2), lax.rem(s // 2, 2)
    later = 0 if backward else 1
    base = quad_ref[...].astype(F32) + jnp.where(z == later, pair_ref[...].astype(F32), 0.0)
    mine_ref[...] = (base + jnp.where(y == later, got_ref[...].astype(F32), 0.0)).astype(BF16)
    theirs_ref[...] = (base + jnp.where(y == later, 0.0, keep_ref[...])).astype(BF16)


def whole_state(refs):
    if len(refs) == 1:
        return refs[0]
    mine_ref, other_ref, all_ref = refs
    y = lax.rem(lax.axis_index("seq"), 2)
    half = mine_ref.shape[0]
    all_ref[lanes(y, half), :] = mine_ref[...]
    all_ref[lanes(1 - y, half), :] = other_ref[...]
    return all_ref


def scan_kernel(count, backward, i_ref, o_ref):
    rows = i_ref.shape[0] // count
    total = jnp.zeros((rows, i_ref.shape[1]), F32)
    order = range(count)
    for c in reversed(order) if backward else order:
        block = pl.ds(c * rows, rows)
        o_ref[block, :] = total.astype(BF16)
        total = total + i_ref[block, :].astype(F32)


def query_grad_kernel(factor, heads, states, k_ref, v_ref, g_ref, *refs):
    o_refs = refs[states : len(refs) - states + 1]
    p_ref = whole_state(refs[:states] + refs[len(refs) - states + 1 :])
    mask = causal(k_ref.shape[0])
    d = lax.axis_index("dp")
    per = heads // len(o_refs)
    for step, o_ref in enumerate(o_refs):
        base = jnp.bitwise_xor(d, step) * per
        for j in range(per):
            cols = lanes(base + j)
            g = g_ref[:, cols]
            grad_scores = scores(g, v_ref[:, cols], mask, factor)
            o_ref[:, pl.ds(j * DH, DH)] = (
                dot(grad_scores, k_ref[:, cols], (1, 0))
                + factor * dot(g, p_ref[cols, :], (1, 1))
            ).astype(BF16)


def attended_kernel(factor, heads, states, shards, inter, count, *refs):
    q_refs, (k_ref, v_ref), refs = refs[:count], refs[count : count + 2], refs[count + 2 :]
    o_ref = refs[states]
    p_ref = whole_state(refs[:states] + refs[states + 1 :])
    mask = causal(k_ref.shape[0])
    for slot in range(heads):
        ref = q_refs[slot * count // heads]
        cols = lanes(head_of(slot, shards, inter))
        q = ref[:, pl.ds(slot % (heads // count) * DH, DH)]
        key_scores = scores(q, k_ref[:, cols], mask, factor)
        o_ref[:, cols] = (
            dot(key_scores, v_ref[:, cols], (1, 0)) + factor * dot(q, p_ref[cols, :], (1, 0))
        ).astype(BF16)


def pair_grad_kernel(factor, heads, states, shards, inter, count, *refs):
    q_refs, (k_ref, v_ref, g_ref), refs = refs[:count], refs[count : count + 3], refs[count + 3 :]
    dk_ref, dv_ref = refs[states : states + 2]
    s_ref = whole_state(refs[:states] + refs[states + 2 :])
    mask = causal(k_ref.shape[0])
    for slot in range(heads):
        ref = q_refs[slot * count // heads]
        cols = lanes(head_of(slot, shards, inter))
        q = ref[:, pl.ds(slot % (heads // count) * DH, DH)]
        k, v, g, suffix = k_ref[:, cols], v_ref[:, cols], g_ref[:, cols], s_ref[cols, :]
        key_scores = scores(q, k, mask, factor)
        grad_scores = scores(g, v, mask, factor)
        dk_ref[:, cols] = (
            dot(grad_scores, q, (0, 0)) + factor * dot(v, suffix, (1, 1))
        ).astype(BF16)
        dv_ref[:, cols] = (
            dot(key_scores, g, (0, 0)) + factor * dot(k, suffix, (1, 0))
        ).astype(BF16)


def project_kernel(mine_ref, theirs_ref, near_ref, far_ref, qa_ref, qb_ref):
    depth = near_ref.shape[1]
    c = lax.rem(lax.axis_index("dp"), 2)
    width = near_ref.shape[2]
    for t_ref, o_ref in ((mine_ref, qa_ref), (theirs_ref, qb_ref)):
        near = t_ref[:, lanes(c, depth)]
        far = t_ref[:, lanes(1 - c, depth)]
        for step in range(near_ref.shape[0]):
            o_ref[:, pl.ds(step * width, width)] = (
                dot(near, near_ref[step], (1, 0)) + dot(far, far_ref[step], (1, 0))
            ).astype(BF16)


def weight_kernel(count, other, steps, *refs):
    o_ref = refs[-1]
    pairs = len(refs) // 2
    rows = refs[0].shape[1] // count
    s = lax.axis_index("seq")
    for place, step in enumerate(steps):
        target = jnp.bitwise_xor(s, step * 2 + other)
        total = None
        for t_ref, g_ref in zip(refs[:pairs], refs[pairs:-1]):
            term = dot(t_ref[:, lanes(target, rows)], g_ref[...], (0, 0))
            total = term if total is None else total + term
        o_ref[pl.ds(place * rows, rows), :] = total.astype(o_ref.dtype)


def fold_kernel(keep_ref, got_ref, o_ref):
    rows = o_ref.shape[0]
    o_ref[...] = (keep_ref[pl.ds(0, rows), :] + got_ref[...].astype(F32)).astype(BF16)


def cross_kernel(keep_ref, got_ref, pair_ref, far_ref, near_ref):
    rows = far_ref.shape[0]
    kept = keep_ref.shape[0] - 2 * rows
    for place, o_ref in enumerate((far_ref, near_ref)):
        o_ref[...] = (
            keep_ref[pl.ds(kept + place * rows, rows), :]
            + got_ref[pl.ds(place * rows, rows), :].astype(F32)
            + pair_ref[pl.ds((1 - place) * rows, rows), :].astype(F32)
        ).astype(o_ref.dtype)


def sum_kernel(first_ref, *refs):
    total = first_ref[...]
    for ref in refs[:-1]:
        total = total + ref[...].astype(F32)
    refs[-1][...] = total.astype(refs[-1].dtype)


def join_kernel(*refs):
    d = lax.axis_index("dp")
    width = refs[0].shape[1]
    for step, ref in enumerate(refs[:-1]):
        refs[-1][:, lanes(jnp.bitwise_xor(d, step), width)] = ref[...].astype(F32)


def body(tokens, query_weight, key_rows, value_rows, out_grad):
    rows, width = key_rows.shape[1:]
    model = tokens.shape[2]
    heads = width // DH
    seqs, dps = lax.axis_size("seq"), lax.axis_size("dp")
    factor = 1.0 / math.sqrt(DH * rows * seqs)
    split = splits(query_weight.shape[1], seqs, dps)
    toks, keys, values, grads = tokens[0], key_rows[0], value_rows[0], out_grad[0]
    state = out((heads * DH, DH), BF16)

    def xor_dp(value, step):
        return lax.ppermute(value, "dp", [(i, i ^ step) for i in range(dps)])

    def flip_seq(value, bits=1):
        return lax.ppermute(value, "seq", [(i, i ^ bits) for i in range(seqs)])

    def swap(value):
        return lax.all_to_all(value, "seq", 0, 0, tiled=True)

    def carried(blocks, backward):
        if not split:
            scan = functools.partial(scan_kernel, seqs, backward)
            got = swap(blocks[0])
            return [swap(call(scan, [state], got)[0])]
        keep, send = blocks
        part = out(send.shape, BF16)
        got = flip_seq(send)
        pair = call(pair_kernel, [part], keep, got)[0]
        pair = flip_seq(pair, 2)
        quad = call(quad_kernel, [part], keep, got, pair)[0]
        low, high = range(4), range(4, 8)
        quad = lax.ppermute(
            quad, "seq", list(zip(high, low) if backward else zip(low, high))
        )
        mine, theirs = call(
            functools.partial(carry_kernel, backward), [part, part], keep, got, pair, quad
        )
        return [mine, flip_seq(theirs)]

    half_state = (heads * DH // 2, DH)
    halves = [out(half_state, F32), out(half_state, BF16)] if split else [state]
    scratch = [state] if split else []
    states = len(halves)

    group = [toks] + [xor_dp(toks, step) for step in (1, 2) if step < dps]
    if split:
        group.append(xor_dp(group[2], 1))
    else:
        group += [xor_dp(toks, step) for step in range(3, dps)]

    block_kv = call(functools.partial(kv_kernel, heads), halves, keys, values)
    prefix = carried(block_kv, False)

    if split:
        d = lax.axis_index("dp")
        half = model // 2
        piece = lax.dynamic_slice(query_weight, (d % 2 * half, d // 2 * DH), (half, DH))
        column = [piece, flip_seq(piece, 2), flip_seq(piece, 4)]
        column.append(flip_seq(column[2], 2))
        sides = [flip_seq(value) for value in column]
        mine, theirs = [], []
        for part in range(2):
            cut = slice(2 * part, 2 * part + 2)
            near = jnp.stack(
                [jnp.concatenate(two, axis=1) for two in zip(column[cut], sides[cut])]
            )
            qs = call(
                project_kernel,
                [out((rows, width // 4), BF16)] * 2,
                toks,
                group[2],
                near,
                xor_dp(near, 1),
                flops=rows * model * width,
            )
            mine.append(qs[0])
            theirs.append(xor_dp(qs[1], 2))
        pair = (*mine, *theirs)
    else:
        query_rows = jnp.dot(
            toks,
            lax.all_gather(query_weight, "seq", axis=1, tiled=True),
            preferred_element_type=F32,
        ).astype(BF16)
        pair = (query_rows[:, : width // 2], query_rows[:, width // 2 :])

    grad_parts = call(
        functools.partial(query_grad_kernel, factor, heads, states),
        [out((rows, width // dps), BF16)] * dps,
        keys,
        values,
        grads,
        *prefix,
        scratch=scratch,
    )
    grad_group = [grad_parts[0]] + [xor_dp(grad_parts[step], step) for step in range(1, dps)]

    if split:
        block = (model // seqs, width // dps)
        cuts = ((1, 3), (2, 0))
        weights = (*group, *grad_group)
        gots = []
        for steps in cuts:
            send = call(
                functools.partial(weight_kernel, seqs, 1, steps),
                [out((len(steps) * block[0], block[1]), BF16)],
                *weights,
            )[0]
            gots.append(flip_seq(send))
        keep = call(
            functools.partial(weight_kernel, seqs, 0, sum(cuts, ())),
            [out((model // 2, block[1]), F32)],
            *weights,
        )[0]
        near = call(fold_kernel, [out((2 * block[0], block[1]), BF16)], keep, gots[0])[0]
        folded = call(
            cross_kernel, [out(block, BF16), out(block, F32)], keep, gots[1], flip_seq(near, 2)
        )
        share = call(sum_kernel, [out(block, BF16)], folded[1], flip_seq(folded[0], 4))[0]
    else:
        share = lax.psum_scatter(
            lax.dot_general(
                jnp.concatenate(group),
                jnp.concatenate(grad_group),
                (((0,), (0,)), ((), ())),
                preferred_element_type=F32,
            ),
            "seq",
            scatter_dimension=0,
            tiled=True,
        )
    weight_grad = call(
        join_kernel,
        [out((share.shape[0], width), F32)],
        share,
        *[xor_dp(share, step) for step in range(1, dps)],
    )[0]

    block_qg = call(
        functools.partial(qg_kernel, heads, seqs, split, len(pair)),
        halves,
        *pair,
        grads,
        scratch=[out((heads * DH, DH), F32)] if split else [],
    )
    suffix = carried(block_qg, True)
    attended = call(
        functools.partial(attended_kernel, factor, heads, states, seqs, split, len(pair)),
        [out((rows, width), BF16)],
        *pair,
        keys,
        values,
        *prefix,
        scratch=scratch,
    )[0]
    key_grad, value_grad = call(
        functools.partial(pair_grad_kernel, factor, heads, states, seqs, split, len(pair)),
        [out((rows, width), BF16)] * 2,
        *pair,
        keys,
        values,
        grads,
        *suffix,
        scratch=scratch,
    )
    return (attended[None], key_grad[None], value_grad[None], weight_grad)


def splits(columns, seqs, dps):
    return columns == 2 * DH and seqs == 8 and dps == 4


def solution(mesh):
    step = jax.shard_map(
        body,
        mesh=mesh,
        in_specs=(
            P("dp", "seq", None),
            P(None, "seq"),
            P("dp", "seq", None),
            P("dp", "seq", None),
            P("dp", "seq", None),
        ),
        out_specs=(
            P("dp", "seq", None),
            P("dp", "seq", None),
            P("dp", "seq", None),
            P("seq", None),
        ),
        check_vma=False,
    )
    if dict(mesh.shape) == {"seq": 8, "dp": 4}:
        return step
    return step
```

```python
import functools
import math

import jax
import jax.numpy as jnp
from jax import lax
from jax.experimental import pallas as pl
from jax.experimental.pallas import tpu as pltpu
from jax.sharding import PartitionSpec as P


DH = 128
F32 = jnp.float32
BF16 = jnp.bfloat16
MIB = 1 << 20


def dot(a, b, dims):
    return lax.dot_general(a, b, ((dims[:1], dims[1:]), ((), ())), preferred_element_type=F32)


def lanes(index, width=DH):
    return pl.ds(pl.multiple_of(index * width, DH), width)


def call(kernel, outs, *args, flops=0, scratch=()):
    moved = sum(math.prod(a.shape) * a.dtype.itemsize for a in (*args, *outs))
    return pl.pallas_call(
        kernel,
        out_shape=tuple(outs),
        in_specs=[pl.BlockSpec(memory_space=pltpu.VMEM)] * len(args),
        out_specs=tuple([pl.BlockSpec(memory_space=pltpu.VMEM)] * len(outs)),
        scratch_shapes=[pltpu.VMEM(a.shape, a.dtype) for a in scratch],
        cost_estimate=pl.CostEstimate(flops=flops, bytes_accessed=moved, transcendentals=0),
        compiler_params=pltpu.CompilerParams(vmem_limit_bytes=min(60 * MIB, 2 * moved + 8 * MIB)),
    )(*args)


def out(shape, dtype):
    return jax.ShapeDtypeStruct(shape, dtype)


def causal(rows):
    return lax.broadcasted_iota(jnp.int32, (rows, rows), 0) >= lax.broadcasted_iota(
        jnp.int32, (rows, rows), 1
    )


def scores(a, b, mask, factor):
    return jnp.where(mask, factor * dot(a, b, (1, 1)), 0.0).astype(BF16)


def head_of(slot, shards, interleaved):
    if not interleaved:
        return slot
    s, d = lax.axis_index("seq"), lax.axis_index("dp")
    half, rest = divmod(slot, shards)
    step, side = divmod(rest, 2)
    source = jnp.bitwise_xor(s, step * 2 + side)
    return source * 2 + lax.rem(d // 2 + half, 2)


def kv_kernel(heads, k_ref, v_ref, *o_refs):
    y = lax.rem(lax.axis_index("seq"), 2)
    per = heads // len(o_refs)
    for part, o_ref in enumerate(o_refs):
        for j in range(per):
            h = j if len(o_refs) == 1 else lax.rem(y + part, 2) * per + j
            cols = lanes(h)
            o_ref[pl.ds(j * DH, DH), :] = dot(k_ref[:, cols], v_ref[:, cols], (0, 0)).astype(
                o_ref.dtype
            )


def qg_kernel(heads, shards, inter, count, *refs):
    q_refs, g_ref, o_refs = refs[:count], refs[count], refs[count + 1 :]
    y = lax.rem(lax.axis_index("seq"), 2)
    total_ref = o_refs[-1]
    for slot in range(heads):
        ref = q_refs[slot * count // heads]
        h = head_of(slot, shards, inter)
        q = ref[:, pl.ds(slot % (heads // count) * DH, DH)]
        total_ref[lanes(h), :] = dot(q, g_ref[:, lanes(h)], (0, 0)).astype(total_ref.dtype)
    half = total_ref.shape[0] // 2
    for part, o_ref in enumerate(o_refs[:-1]):
        o_ref[...] = total_ref[lanes(lax.rem(y + part, 2), half), :].astype(o_ref.dtype)


def pair_kernel(keep_ref, got_ref, o_ref):
    o_ref[...] = (keep_ref[...] + got_ref[...].astype(F32)).astype(BF16)


def quad_kernel(keep_ref, got_ref, pair_ref, o_ref):
    o_ref[...] = (
        keep_ref[...] + got_ref[...].astype(F32) + pair_ref[...].astype(F32)
    ).astype(BF16)


def carry_kernel(backward, keep_ref, got_ref, pair_ref, quad_ref, mine_ref, theirs_ref):
    s = lax.axis_index("seq")
    y, z = lax.rem(s, 2), lax.rem(s // 2, 2)
    later = 0 if backward else 1
    base = quad_ref[...].astype(F32) + jnp.where(z == later, pair_ref[...].astype(F32), 0.0)
    mine_ref[...] = (base + jnp.where(y == later, got_ref[...].astype(F32), 0.0)).astype(BF16)
    theirs_ref[...] = (base + jnp.where(y == later, 0.0, keep_ref[...])).astype(BF16)


def whole_state(refs):
    if len(refs) == 1:
        return refs[0]
    mine_ref, other_ref, all_ref = refs
    y = lax.rem(lax.axis_index("seq"), 2)
    half = mine_ref.shape[0]
    all_ref[lanes(y, half), :] = mine_ref[...]
    all_ref[lanes(1 - y, half), :] = other_ref[...]
    return all_ref


def scan_kernel(count, backward, i_ref, o_ref):
    rows = i_ref.shape[0] // count
    total = jnp.zeros((rows, i_ref.shape[1]), F32)
    order = range(count)
    for c in reversed(order) if backward else order:
        block = pl.ds(c * rows, rows)
        o_ref[block, :] = total.astype(BF16)
        total = total + i_ref[block, :].astype(F32)


def query_grad_kernel(factor, heads, states, k_ref, v_ref, g_ref, *refs):
    o_refs = refs[states : len(refs) - states + 1]
    p_ref = whole_state(refs[:states] + refs[len(refs) - states + 1 :])
    mask = causal(k_ref.shape[0])
    d = lax.axis_index("dp")
    per = heads // len(o_refs)
    for step, o_ref in enumerate(o_refs):
        base = jnp.bitwise_xor(d, step) * per
        for j in range(per):
            cols = lanes(base + j)
            g = g_ref[:, cols]
            grad_scores = scores(g, v_ref[:, cols], mask, factor)
            o_ref[:, pl.ds(j * DH, DH)] = (
                dot(grad_scores, k_ref[:, cols], (1, 0))
                + factor * dot(g, p_ref[cols, :], (1, 1))
            ).astype(BF16)


def attended_kernel(factor, heads, states, shards, inter, count, *refs):
    q_refs, (k_ref, v_ref), refs = refs[:count], refs[count : count + 2], refs[count + 2 :]
    o_ref = refs[states]
    p_ref = whole_state(refs[:states] + refs[states + 1 :])
    mask = causal(k_ref.shape[0])
    for slot in range(heads):
        ref = q_refs[slot * count // heads]
        cols = lanes(head_of(slot, shards, inter))
        q = ref[:, pl.ds(slot % (heads // count) * DH, DH)]
        key_scores = scores(q, k_ref[:, cols], mask, factor)
        o_ref[:, cols] = (
            dot(key_scores, v_ref[:, cols], (1, 0)) + factor * dot(q, p_ref[cols, :], (1, 0))
        ).astype(BF16)


def key_grad_kernel(factor, heads, states, shards, inter, count, *refs):
    q_refs, (v_ref, g_ref), refs = refs[:count], refs[count : count + 2], refs[count + 2 :]
    o_ref = refs[states]
    s_ref = whole_state(refs[:states] + refs[states + 1 :])
    mask = causal(v_ref.shape[0])
    for slot in range(heads):
        ref = q_refs[slot * count // heads]
        cols = lanes(head_of(slot, shards, inter))
        q = ref[:, pl.ds(slot % (heads // count) * DH, DH)]
        v = v_ref[:, cols]
        grad_scores = scores(g_ref[:, cols], v, mask, factor)
        o_ref[:, cols] = (
            dot(grad_scores, q, (0, 0)) + factor * dot(v, s_ref[cols, :], (1, 1))
        ).astype(BF16)


def value_grad_kernel(factor, heads, states, shards, inter, count, *refs):
    q_refs, (k_ref, g_ref), refs = refs[:count], refs[count : count + 2], refs[count + 2 :]
    o_ref = refs[states]
    s_ref = whole_state(refs[:states] + refs[states + 1 :])
    mask = causal(k_ref.shape[0])
    for slot in range(heads):
        ref = q_refs[slot * count // heads]
        cols = lanes(head_of(slot, shards, inter))
        q = ref[:, pl.ds(slot % (heads // count) * DH, DH)]
        k = k_ref[:, cols]
        key_scores = scores(q, k, mask, factor)
        o_ref[:, cols] = (
            dot(key_scores, g_ref[:, cols], (0, 0)) + factor * dot(k, s_ref[cols, :], (1, 0))
        ).astype(BF16)


def project_kernel(mine_ref, theirs_ref, near_ref, far_ref, qa_ref, qb_ref):
    depth = near_ref.shape[1]
    c = lax.rem(lax.axis_index("dp"), 2)
    width = near_ref.shape[2]
    for t_ref, o_ref in ((mine_ref, qa_ref), (theirs_ref, qb_ref)):
        near = t_ref[:, lanes(c, depth)]
        far = t_ref[:, lanes(1 - c, depth)]
        for step in range(near_ref.shape[0]):
            o_ref[:, pl.ds(step * width, width)] = (
                dot(near, near_ref[step], (1, 0)) + dot(far, far_ref[step], (1, 0))
            ).astype(BF16)


def weight_kernel(count, pairs, other, steps, *refs):
    rows = refs[0].shape[1] // count
    s = lax.axis_index("seq")
    for step, o_ref in zip(steps, refs[2 * pairs :]):
        target = jnp.bitwise_xor(s, step * 2 + other)
        total = None
        for t_ref, g_ref in zip(refs[:pairs], refs[pairs : 2 * pairs]):
            term = dot(t_ref[:, lanes(target, rows)], g_ref[...], (0, 0))
            total = term if total is None else total + term
        o_ref[...] = total.astype(o_ref.dtype)


def sum_kernel(first_ref, *refs):
    total = first_ref[...]
    for ref in refs[:-1]:
        total = total + ref[...].astype(F32)
    refs[-1][...] = total.astype(refs[-1].dtype)


def join_kernel(*refs):
    d = lax.axis_index("dp")
    width = refs[0].shape[1]
    for step, ref in enumerate(refs[:-1]):
        refs[-1][:, lanes(jnp.bitwise_xor(d, step), width)] = ref[...].astype(F32)


def body(tokens, query_weight, key_rows, value_rows, out_grad):
    rows, width = key_rows.shape[1:]
    model = tokens.shape[2]
    heads = width // DH
    seqs, dps = lax.axis_size("seq"), lax.axis_size("dp")
    factor = 1.0 / math.sqrt(DH * rows * seqs)
    split = splits(query_weight.shape[1], seqs, dps)
    toks, keys, values, grads = tokens[0], key_rows[0], value_rows[0], out_grad[0]
    state = out((heads * DH, DH), BF16)

    def xor_dp(value, step):
        return lax.ppermute(value, "dp", [(i, i ^ step) for i in range(dps)])

    def flip_seq(value, bits=1):
        return lax.ppermute(value, "seq", [(i, i ^ bits) for i in range(seqs)])

    def swap(value):
        return lax.all_to_all(value, "seq", 0, 0, tiled=True)

    def carried(blocks, backward):
        if not split:
            scan = functools.partial(scan_kernel, seqs, backward)
            got = swap(blocks[0])
            return [swap(call(scan, [state], got)[0])]
        keep, send = blocks
        part = out(send.shape, BF16)
        got = flip_seq(send)
        pair = call(pair_kernel, [part], keep, got)[0]
        pair = flip_seq(pair, 2)
        quad = call(quad_kernel, [part], keep, got, pair)[0]
        low, high = range(4), range(4, 8)
        quad = lax.ppermute(
            quad, "seq", list(zip(high, low) if backward else zip(low, high))
        )
        mine, theirs = call(
            functools.partial(carry_kernel, backward), [part, part], keep, got, pair, quad
        )
        return [mine, flip_seq(theirs)]

    half_state = (heads * DH // 2, DH)
    halves = [out(half_state, F32), out(half_state, BF16)] if split else [state]
    scratch = [state] if split else []
    states = len(halves)

    group = [toks] + [xor_dp(toks, step) for step in (1, 2) if step < dps]
    if split:
        group.append(xor_dp(group[2], 1))
    else:
        group += [xor_dp(toks, step) for step in range(3, dps)]

    block_kv = call(functools.partial(kv_kernel, heads), halves, keys, values)
    prefix = carried(block_kv, False)

    if split:
        d = lax.axis_index("dp")
        half = model // 2
        piece = lax.dynamic_slice(query_weight, (d % 2 * half, d // 2 * DH), (half, DH))
        column = [piece, flip_seq(piece, 2), flip_seq(piece, 4)]
        column.append(flip_seq(column[2], 2))
        sides = [flip_seq(value) for value in column]
        mine, theirs = [], []
        for part in range(2):
            cut = slice(2 * part, 2 * part + 2)
            near = jnp.stack(
                [jnp.concatenate(two, axis=1) for two in zip(column[cut], sides[cut])]
            )
            qs = call(
                project_kernel,
                [out((rows, width // 4), BF16)] * 2,
                toks,
                group[2],
                near,
                xor_dp(near, 1),
                flops=rows * model * width,
            )
            mine.append(qs[0])
            theirs.append(xor_dp(qs[1], 2))
        pair = (*mine, *theirs)
    else:
        query_rows = jnp.dot(
            toks,
            lax.all_gather(query_weight, "seq", axis=1, tiled=True),
            preferred_element_type=F32,
        ).astype(BF16)
        pair = (query_rows[:, : width // 2], query_rows[:, width // 2 :])

    grad_parts = call(
        functools.partial(query_grad_kernel, factor, heads, states),
        [out((rows, width // dps), BF16)] * dps,
        keys,
        values,
        grads,
        *prefix,
        scratch=scratch,
    )
    grad_group = [grad_parts[0]] + [xor_dp(grad_parts[step], step) for step in range(1, dps)]

    if split:
        block = (model // seqs, width // dps)
        weights = (*group, *grad_group)

        def formed(other, steps, dtype):
            kernel = functools.partial(weight_kernel, seqs, dps, other, steps)
            return dict(zip(steps, call(kernel, [out(block, dtype)] * len(steps), *weights)))

        def added(dtype, *terms):
            return call(sum_kernel, [out(block, dtype)], *terms)[0]

        order = (3, 2, 1, 0)
        sends = {**formed(1, order[:1], BF16), **formed(1, order[1:], BF16)}
        got = {step: flip_seq(sends[step]) for step in order}
        keep = formed(0, order, F32)
        near = flip_seq(added(BF16, keep[3], got[3]), 2)
        cross = flip_seq(added(BF16, keep[2], got[2], near), 4)
        near = flip_seq(added(BF16, keep[1], got[1]), 2)
        share = added(BF16, keep[0], got[0], near, cross)
    else:
        share = lax.psum_scatter(
            lax.dot_general(
                jnp.concatenate(group),
                jnp.concatenate(grad_group),
                (((0,), (0,)), ((), ())),
                preferred_element_type=F32,
            ),
            "seq",
            scatter_dimension=0,
            tiled=True,
        )
    shares = [share] + [xor_dp(share, step) for step in (1, 2) if step < dps]
    if split:
        shares.append(xor_dp(shares[2], 1))
    else:
        shares += [xor_dp(share, step) for step in range(3, dps)]
    weight_grad = call(join_kernel, [out((share.shape[0], width), F32)], *shares)[0]

    block_qg = call(
        functools.partial(qg_kernel, heads, seqs, split, len(pair)),
        halves,
        *pair,
        grads,
        scratch=[out((heads * DH, DH), F32)] if split else [],
    )
    suffix = carried(block_qg, True)
    attended = call(
        functools.partial(attended_kernel, factor, heads, states, seqs, split, len(pair)),
        [out((rows, width), BF16)],
        *pair,
        keys,
        values,
        *prefix,
        scratch=scratch,
    )[0]
    key_grad, value_grad = (
        call(
            functools.partial(kernel, factor, heads, states, seqs, split, len(pair)),
            [out((rows, width), BF16)],
            *pair,
            operand,
            grads,
            *suffix,
            scratch=scratch,
        )[0]
        for kernel, operand in ((key_grad_kernel, values), (value_grad_kernel, keys))
    )
    return (attended[None], key_grad[None], value_grad[None], weight_grad)


def splits(columns, seqs, dps):
    return columns == 2 * DH and seqs == 8 and dps == 4


def solution(mesh):
    step = jax.shard_map(
        body,
        mesh=mesh,
        in_specs=(
            P("dp", "seq", None),
            P(None, "seq"),
            P("dp", "seq", None),
            P("dp", "seq", None),
            P("dp", "seq", None),
        ),
        out_specs=(
            P("dp", "seq", None),
            P("dp", "seq", None),
            P("dp", "seq", None),
            P("seq", None),
        ),
        check_vma=False,
    )
    if dict(mesh.shape) == {"seq": 8, "dp": 4}:
        return step
    return step
```

```python
import functools
import math

import jax
import jax.numpy as jnp
from jax import lax
from jax.experimental import pallas as pl
from jax.experimental.pallas import tpu as pltpu
from jax.sharding import PartitionSpec as P


DH = 128
F32 = jnp.float32
BF16 = jnp.bfloat16
MIB = 1 << 20


def dot(a, b, dims):
    return lax.dot_general(a, b, ((dims[:1], dims[1:]), ((), ())), preferred_element_type=F32)


def lanes(index, width=DH):
    return pl.ds(pl.multiple_of(index * width, DH), width)


def call(kernel, outs, *args, flops=0, scratch=()):
    moved = sum(math.prod(a.shape) * a.dtype.itemsize for a in (*args, *outs))
    return pl.pallas_call(
        kernel,
        out_shape=tuple(outs),
        in_specs=[pl.BlockSpec(memory_space=pltpu.VMEM)] * len(args),
        out_specs=tuple([pl.BlockSpec(memory_space=pltpu.VMEM)] * len(outs)),
        scratch_shapes=[pltpu.VMEM(a.shape, a.dtype) for a in scratch],
        cost_estimate=pl.CostEstimate(flops=flops, bytes_accessed=moved, transcendentals=0),
        compiler_params=pltpu.CompilerParams(vmem_limit_bytes=min(60 * MIB, 2 * moved + 8 * MIB)),
    )(*args)


def out(shape, dtype):
    return jax.ShapeDtypeStruct(shape, dtype)


def causal(rows, query_axis=0):
    axes = [lax.broadcasted_iota(jnp.int32, (rows, rows), axis) for axis in (0, 1)]
    return axes[query_axis] >= axes[1 - query_axis]


def scores(a, b, mask, factor):
    return jnp.where(mask, factor * dot(a, b, (1, 1)), 0.0).astype(BF16)


def head_of(slot, shards, interleaved):
    if not interleaved:
        return slot
    s, d = lax.axis_index("seq"), lax.axis_index("dp")
    half, rest = divmod(slot, shards)
    step, side = divmod(rest, 2)
    source = jnp.bitwise_xor(s, step * 2 + side)
    return source * 2 + lax.rem(d // 2 + half, 2)


def kv_kernel(heads, k_ref, v_ref, *o_refs):
    y = lax.rem(lax.axis_index("seq"), 2)
    per = heads // len(o_refs)
    for part, o_ref in enumerate(o_refs):
        for j in range(per):
            h = j if len(o_refs) == 1 else lax.rem(y + part, 2) * per + j
            cols = lanes(h)
            o_ref[pl.ds(j * DH, DH), :] = dot(k_ref[:, cols], v_ref[:, cols], (0, 0)).astype(
                o_ref.dtype
            )


def qg_kernel(heads, shards, inter, count, *refs):
    q_refs, g_ref, o_refs = refs[:count], refs[count], refs[count + 1 :]
    y = lax.rem(lax.axis_index("seq"), 2)
    total_ref = o_refs[-1]
    for slot in range(heads):
        ref = q_refs[slot * count // heads]
        h = head_of(slot, shards, inter)
        q = ref[:, pl.ds(slot % (heads // count) * DH, DH)]
        total_ref[lanes(h), :] = dot(q, g_ref[:, lanes(h)], (0, 0)).astype(total_ref.dtype)
    half = total_ref.shape[0] // 2
    for part, o_ref in enumerate(o_refs[:-1]):
        o_ref[...] = total_ref[lanes(lax.rem(y + part, 2), half), :].astype(o_ref.dtype)


def pair_kernel(keep_ref, got_ref, o_ref):
    o_ref[...] = (keep_ref[...] + got_ref[...].astype(F32)).astype(BF16)


def quad_kernel(keep_ref, got_ref, pair_ref, o_ref):
    z = lax.rem(lax.axis_index("seq") // 2, 2)
    rows = o_ref.shape[0]
    if rows == keep_ref.shape[0]:
        part = pl.ds(0, rows)
    else:
        part = lanes(z, rows)
    o_ref[...] = (
        keep_ref[part, :] + got_ref[part, :].astype(F32) + pair_ref[part, :].astype(F32)
    ).astype(BF16)


def carry_kernel(backward, keep_ref, got_ref, pair_ref, *refs):
    *quad_refs, mine_ref, theirs_ref = refs
    s = lax.axis_index("seq")
    y, z = lax.rem(s, 2), lax.rem(s // 2, 2)
    later = 0 if backward else 1
    rows = quad_refs[0].shape[0]
    for n, quad_ref in enumerate(quad_refs):
        part = pl.ds(0, rows) if len(quad_refs) == 1 else lanes(lax.rem(z + n, 2), rows)
        base = quad_ref[...].astype(F32) + jnp.where(
            z == later, pair_ref[part, :].astype(F32), 0.0
        )
        mine_ref[part, :] = (
            base + jnp.where(y == later, got_ref[part, :].astype(F32), 0.0)
        ).astype(BF16)
        theirs_ref[part, :] = (base + jnp.where(y == later, 0.0, keep_ref[part, :])).astype(BF16)


def whole_state(refs):
    if len(refs) == 1:
        return refs[0]
    mine_ref, other_ref, all_ref = refs
    y = lax.rem(lax.axis_index("seq"), 2)
    half = mine_ref.shape[0]
    all_ref[lanes(y, half), :] = mine_ref[...]
    all_ref[lanes(1 - y, half), :] = other_ref[...]
    return all_ref


def scan_kernel(count, backward, i_ref, o_ref):
    rows = i_ref.shape[0] // count
    total = jnp.zeros((rows, i_ref.shape[1]), F32)
    order = range(count)
    for c in reversed(order) if backward else order:
        block = pl.ds(c * rows, rows)
        o_ref[block, :] = total.astype(BF16)
        total = total + i_ref[block, :].astype(F32)


def query_grad_kernel(factor, heads, states, part, parts, k_ref, v_ref, g_ref, *refs):
    o_refs = refs[states : len(refs) - states + 1]
    p_ref = whole_state(refs[:states] + refs[len(refs) - states + 1 :])
    mask = causal(k_ref.shape[0])
    d = lax.axis_index("dp")
    per = heads // len(o_refs) // parts
    for step, o_ref in enumerate(o_refs):
        base = (jnp.bitwise_xor(d, step) * parts + part) * per
        for j in range(per):
            cols = lanes(base + j)
            g = g_ref[:, cols]
            grad_scores = scores(g, v_ref[:, cols], mask, factor)
            o_ref[:, pl.ds(j * DH, DH)] = (
                dot(grad_scores, k_ref[:, cols], (1, 0))
                + factor * dot(g, p_ref[cols, :], (1, 1))
            ).astype(BF16)


def attended_kernel(factor, heads, states, shards, inter, count, *refs):
    q_refs, (k_ref, v_ref), refs = refs[:count], refs[count : count + 2], refs[count + 2 :]
    o_ref = refs[states]
    p_ref = whole_state(refs[:states] + refs[states + 1 :])
    mask = causal(k_ref.shape[0])
    for slot in range(heads):
        ref = q_refs[slot * count // heads]
        cols = lanes(head_of(slot, shards, inter))
        q = ref[:, pl.ds(slot % (heads // count) * DH, DH)]
        key_scores = scores(q, k_ref[:, cols], mask, factor)
        o_ref[:, cols] = (
            dot(key_scores, v_ref[:, cols], (1, 0)) + factor * dot(q, p_ref[cols, :], (1, 0))
        ).astype(BF16)


def key_grad_kernel(factor, heads, states, shards, inter, count, *refs):
    q_refs, (v_ref, g_ref), refs = refs[:count], refs[count : count + 2], refs[count + 2 :]
    o_ref = refs[states]
    s_ref = whole_state(refs[:states] + refs[states + 1 :])
    mask = causal(v_ref.shape[0], 1)
    for slot in range(heads):
        ref = q_refs[slot * count // heads]
        cols = lanes(head_of(slot, shards, inter))
        q = ref[:, pl.ds(slot % (heads // count) * DH, DH)]
        v = v_ref[:, cols]
        grad_scores = scores(v, g_ref[:, cols], mask, factor)
        o_ref[:, cols] = (
            dot(grad_scores, q, (1, 0)) + factor * dot(v, s_ref[cols, :], (1, 1))
        ).astype(BF16)


def value_grad_kernel(factor, heads, states, shards, inter, count, *refs):
    q_refs, (k_ref, g_ref), refs = refs[:count], refs[count : count + 2], refs[count + 2 :]
    o_ref = refs[states]
    s_ref = whole_state(refs[:states] + refs[states + 1 :])
    mask = causal(k_ref.shape[0], 1)
    for slot in range(heads):
        ref = q_refs[slot * count // heads]
        cols = lanes(head_of(slot, shards, inter))
        q = ref[:, pl.ds(slot % (heads // count) * DH, DH)]
        k = k_ref[:, cols]
        key_scores = scores(k, q, mask, factor)
        o_ref[:, cols] = (
            dot(key_scores, g_ref[:, cols], (1, 0)) + factor * dot(k, s_ref[cols, :], (1, 0))
        ).astype(BF16)


def project_kernel(mine_ref, theirs_ref, near_ref, far_ref, qa_ref, qb_ref):
    depth = near_ref.shape[1]
    c = lax.rem(lax.axis_index("dp"), 2)
    width = near_ref.shape[2]
    for t_ref, o_ref in ((mine_ref, qa_ref), (theirs_ref, qb_ref)):
        near = t_ref[:, lanes(c, depth)]
        far = t_ref[:, lanes(1 - c, depth)]
        for step in range(near_ref.shape[0]):
            o_ref[:, pl.ds(step * width, width)] = (
                dot(near, near_ref[step], (1, 0)) + dot(far, far_ref[step], (1, 0))
            ).astype(BF16)


def weight_kernel(count, pairs, other, steps, *refs):
    rows = refs[0].shape[1] // count
    s = lax.axis_index("seq")
    t_refs, g_refs, o_ref = refs[:pairs], refs[pairs:-1], refs[-1]
    width = g_refs[0].shape[1]
    for place, step in enumerate(steps):
        target = jnp.bitwise_xor(s, step * 2 + other)
        for part in range(len(g_refs) // pairs):
            total = None
            for t_ref, g_ref in zip(t_refs, g_refs[part * pairs :]):
                term = dot(t_ref[:, lanes(target, rows)], g_ref[...], (0, 0))
                total = term if total is None else total + term
            o_ref[pl.ds(place * rows, rows), pl.ds(part * width, width)] = total.astype(
                o_ref.dtype
            )


def sum_kernel(starts, *refs):
    o_ref = refs[-1]
    rows, width = o_ref.shape
    total = None
    for (row, col), ref in zip(starts, refs[:-1]):
        term = ref[pl.ds(row, rows), pl.ds(col, width)].astype(F32)
        total = term if total is None else total + term
    o_ref[...] = total.astype(o_ref.dtype)


def share_kernel(row, keep_ref, got_ref, near_ref, *refs):
    o_ref = refs[-1]
    rows = o_ref.shape[0]
    width = refs[0].shape[1]
    for part, cross_ref in enumerate(refs[:-1]):
        cols = pl.ds(part * width, width)
        total = keep_ref[pl.ds(row, rows), cols] + got_ref[pl.ds(rows, rows), cols].astype(F32)
        total = total + near_ref[:, cols].astype(F32) + cross_ref[...].astype(F32)
        o_ref[:, cols] = total.astype(o_ref.dtype)


def join_kernel(*refs):
    d = lax.axis_index("dp")
    width = refs[0].shape[1]
    for step, ref in enumerate(refs[:-1]):
        refs[-1][:, lanes(jnp.bitwise_xor(d, step), width)] = ref[...].astype(F32)


HALVED = ("qg",)


def body(tokens, query_weight, key_rows, value_rows, out_grad):
    rows, width = key_rows.shape[1:]
    model = tokens.shape[2]
    heads = width // DH
    seqs, dps = lax.axis_size("seq"), lax.axis_size("dp")
    factor = 1.0 / math.sqrt(DH * rows * seqs)
    split = splits(query_weight.shape[1], seqs, dps)
    toks, keys, values, grads = tokens[0], key_rows[0], value_rows[0], out_grad[0]
    state = out((heads * DH, DH), BF16)

    def xor_dp(value, step):
        return lax.ppermute(value, "dp", [(i, i ^ step) for i in range(dps)])

    def flip_seq(value, bits=1):
        return lax.ppermute(value, "seq", [(i, i ^ bits) for i in range(seqs)])

    def swap(value):
        return lax.all_to_all(value, "seq", 0, 0, tiled=True)

    def carried(name, blocks, backward):
        if not split:
            scan = functools.partial(scan_kernel, seqs, backward)
            got = swap(blocks[0])
            return [swap(call(scan, [state], got)[0])]
        keep, send = blocks
        part = out(send.shape, BF16)
        got = flip_seq(send)
        pair = call(pair_kernel, [part], keep, got)[0]
        pair = flip_seq(pair, 2)
        thin = out((part.shape[0] // 2, DH), BF16) if name in HALVED else part
        quad = call(quad_kernel, [thin], keep, got, pair)[0]
        low, high = range(4), range(4, 8)
        quad = lax.ppermute(
            quad, "seq", list(zip(high, low) if backward else zip(low, high))
        )
        quads = [quad, flip_seq(quad, 2)] if name in HALVED else [quad]
        mine, theirs = call(
            functools.partial(carry_kernel, backward), [part, part], keep, got, pair, *quads
        )
        return [mine, flip_seq(theirs)]

    half_state = (heads * DH // 2, DH)
    halves = [out(half_state, F32), out(half_state, BF16)] if split else [state]
    scratch = [state] if split else []
    states = len(halves)

    group = [toks] + [xor_dp(toks, step) for step in (1, 2) if step < dps]
    if split:
        group.append(xor_dp(group[2], 1))
    else:
        group += [xor_dp(toks, step) for step in range(3, dps)]

    block_kv = call(functools.partial(kv_kernel, heads), halves, keys, values)
    prefix = carried("kv", block_kv, False)

    if split:
        d = lax.axis_index("dp")
        half = model // 2
        piece = lax.dynamic_slice(query_weight, (d % 2 * half, d // 2 * DH), (half, DH))
        column = [piece, flip_seq(piece, 2), flip_seq(piece, 4)]
        column.append(flip_seq(column[2], 2))
        sides = [flip_seq(value) for value in column]
        mine, theirs = [], []
        for part in range(2):
            cut = slice(2 * part, 2 * part + 2)
            near = jnp.stack(
                [jnp.concatenate(two, axis=1) for two in zip(column[cut], sides[cut])]
            )
            qs = call(
                project_kernel,
                [out((rows, width // 4), BF16)] * 2,
                toks,
                group[2],
                near,
                xor_dp(near, 1),
                flops=rows * model * width,
            )
            mine.append(qs[0])
            theirs.append(xor_dp(qs[1], 2))
        pair = (*mine, *theirs)
    else:
        query_rows = jnp.dot(
            toks,
            lax.all_gather(query_weight, "seq", axis=1, tiled=True),
            preferred_element_type=F32,
        ).astype(BF16)
        pair = (query_rows[:, : width // 2], query_rows[:, width // 2 :])

    parts = 2 if split else 1
    grad_groups = []
    for part in range(parts):
        sent = call(
            functools.partial(query_grad_kernel, factor, heads, states, part, parts),
            [out((rows, width // dps // parts), BF16)] * dps,
            keys,
            values,
            grads,
            *prefix,
            scratch=scratch,
        )
        grad_groups.append([sent[0]] + [xor_dp(sent[step], step) for step in range(1, dps)])

    if split:
        block, half = model // seqs, width // dps // 2
        thin, wide = (block, half), (block, 2 * half)

        def formed(other, steps, dtype, *which):
            kernel = functools.partial(weight_kernel, seqs, dps, other, steps)
            shape = (len(steps) * block, len(which) * half)
            terms = sum((grad_groups[part] for part in which), [])
            return call(kernel, [out(shape, dtype)], *group, *terms)[0]

        def added(shape, starts, *terms):
            return call(functools.partial(sum_kernel, starts), [out(shape, BF16)], *terms)[0]

        got = {
            (step, part): flip_seq(formed(1, (step,), BF16, part))
            for part in (0, 1)
            for step in (3, 2)
        }
        rest = flip_seq(formed(1, (1, 0), BF16, 0, 1))
        keep = formed(0, (3, 2, 1, 0), F32, 0, 1)
        zero, crosses = (0, 0), []
        for part in (0, 1):
            near = added(thin, ((0, part * half), zero), keep, got[3, part])
            near = flip_seq(near, 2)
            starts = ((block, part * half), zero, zero)
            far = added(thin, starts, keep, got[2, part], near)
            crosses.append(flip_seq(far, 4))
        near = added(wide, ((2 * block, 0), zero), keep, rest)
        near = flip_seq(near, 2)
        share = call(
            functools.partial(share_kernel, 3 * block),
            [out(wide, BF16)],
            keep,
            rest,
            near,
            *crosses,
        )[0]
    else:
        share = lax.psum_scatter(
            lax.dot_general(
                jnp.concatenate(group),
                jnp.concatenate(grad_groups[0]),
                (((0,), (0,)), ((), ())),
                preferred_element_type=F32,
            ),
            "seq",
            scatter_dimension=0,
            tiled=True,
        )
    shares = [share] + [xor_dp(share, step) for step in (1, 2) if step < dps]
    if split:
        shares.append(xor_dp(shares[2], 1))
    else:
        shares += [xor_dp(share, step) for step in range(3, dps)]
    weight_grad = call(join_kernel, [out((share.shape[0], width), F32)], *shares)[0]

    block_qg = call(
        functools.partial(qg_kernel, heads, seqs, split, len(pair)),
        halves,
        *pair,
        grads,
        scratch=[out((heads * DH, DH), F32)] if split else [],
    )
    suffix = carried("qg", block_qg, True)
    attended = call(
        functools.partial(attended_kernel, factor, heads, states, seqs, split, len(pair)),
        [out((rows, width), BF16)],
        *pair,
        keys,
        values,
        *prefix,
        scratch=scratch,
    )[0]
    key_grad, value_grad = (
        call(
            functools.partial(kernel, factor, heads, states, seqs, split, len(pair)),
            [out((rows, width), BF16)],
            *pair,
            operand,
            grads,
            *suffix,
            scratch=scratch,
        )[0]
        for kernel, operand in ((key_grad_kernel, values), (value_grad_kernel, keys))
    )
    return (attended[None], key_grad[None], value_grad[None], weight_grad)


def splits(columns, seqs, dps):
    return columns == 2 * DH and seqs == 8 and dps == 4


def solution(mesh):
    step = jax.shard_map(
        body,
        mesh=mesh,
        in_specs=(
            P("dp", "seq", None),
            P(None, "seq"),
            P("dp", "seq", None),
            P("dp", "seq", None),
            P("dp", "seq", None),
        ),
        out_specs=(
            P("dp", "seq", None),
            P("dp", "seq", None),
            P("dp", "seq", None),
            P("seq", None),
        ),
        check_vma=False,
    )
    if dict(mesh.shape) == {"seq": 8, "dp": 4}:
        return step
    return step
```
